32 devices in a mesh: dp: 16 (over z, x, core), shard: 2 (over y).
Axes of the slice: x: 2, y: 2, z: 4, core: 2. Of those that a mesh axis runs over, the one named last changes fastest.
Arguments:
- acts: bfloat16 [32768, 4096], P('dp', 'shard'), may hold values from -6 to 6
- grad_out: bfloat16 [32768, 14336], P('dp', 'shard'), may hold values from -15 to 15
- projector: bfloat16 [4096, 512], P('shard'), may hold values from -0.09375 to 0.09375
- weight: bfloat16 [4096, 14336], P('dp', 'shard'), may hold values from -0.09375 to 0.09375
- moment1: float32 [512, 14336], P('dp', 'shard'), may hold values from -24 to 24
- moment2: float32 [512, 14336], P('dp', 'shard'), may hold values from 1 to 16
Outputs:
- new_weight: bfloat16 [4096, 14336], P('dp', 'shard')
- new_moment1: float32 [512, 14336], P('dp', 'shard')
- new_moment2: float32 [512, 14336], P('dp', 'shard')
The draws below stay inside these ranges and needn't reach their ends.
All inputs are finite; a program needn't handle non-finite values.
Results may differ from the reference program's by a relative error of at most 0.005.
Values may be sent and summed in bfloat16 or wider, within the bound.
No kernel may reach another device: no remote copies, remote signals or barrier semaphores. Data moves between devices by JAX's collectives and lax.ppermute only.
A program may use at most 128 MiB of HBM per device.

```python
import math
import jax
import jax.numpy as jnp

D = 4096
FF = 14336
R = 512
TOKENS = 32768


def draw_grad_out(key, part):
    key_noise, key_column = jax.random.split(key, 2)
    column = jnp.arange(FF, dtype=jnp.float32)
    column_scale = jnp.exp(jnp.log(3.0) * column / FF + jax.random.uniform(key_column, (FF,), jnp.float32, 0.0, jnp.log(10.0))) / 8.0
    base = jax.random.truncated_normal(key_noise, -4.0, 4.0, (TOKENS, FF), jnp.float32)
    return (base * column_scale).astype(jnp.bfloat16)


def level_of(stream_key, dims, cuts, smallest, high):
    def one(dim, blocks):
        heights = jax.random.uniform(jax.random.fold_in(jax.random.fold_in(stream_key, 6), dim), (blocks,), jnp.float32, smallest / len(cuts), high / len(cuts))
        return jnp.repeat(jnp.exp(heights), dims[dim] // blocks).reshape((-1,) + (1,) * (len(dims) - dim - 1))

    level = one(*cuts[0])
    for cut in cuts[1:]:
        level = level * one(*cut)
    return level


def centred(stream_key, dims, width, bound, cuts=(), held_as=jnp.bfloat16):
    entries = jax.random.normal(stream_key, dims, jnp.float32) * width
    if len(cuts) > 0:
        entries = level_of(stream_key, dims, cuts, -0.22, 0.18) * entries
    return jnp.clip(entries, min=-bound, max=bound).astype(held_as)


def setup_inputs(seed: int = 0) -> dict:
    seeds = jax.random.split(jax.random.key(seed), 7)
    acts = centred(seeds[0], (TOKENS, D), 1.0, 6.0, ((0, 16), (1, 2)))
    grad_out = draw_grad_out(jax.random.fold_in(seeds[6], 71), 0)
    projector = centred(seeds[2], (D, R), D ** -0.5, 0.09375, ((0, 2),))
    weight = centred(seeds[3], (D, FF), D ** -0.5, 0.09375, ((0, 16), (1, 2)))
    moment1 = centred(seeds[4], (R, FF), 4.0, 24.0, ((0, 16), (1, 2)), jnp.float32)
    moment2 = jnp.clip(jnp.exp(math.log(16.0) - 2.7725887 * jax.random.uniform(seeds[5], (R, FF), jnp.float32) ** level_of(seeds[5], (R, FF), ((0, 16), (1, 2)), -0.2, 0.2)), 1.0, 16.0)
    return dict(acts=acts, grad_out=grad_out, projector=projector, weight=weight, moment1=moment1, moment2=moment2)


first_fix = 0.9999734386011124
second_fix = 0.994079470779666

def reference(acts, grad_out, projector, weight, moment1, moment2):
    projected = jnp.dot(acts, projector, preferred_element_type=jnp.float32).astype(jnp.bfloat16)
    gradient = jnp.dot(projected.T, grad_out, preferred_element_type=jnp.float32)
    root_mean = jnp.sqrt(jnp.sum(gradient * gradient) / (R * FF) + 1e-06)
    clip_factor = jnp.minimum(1.0, 4.0 / root_mean)
    clipped = clip_factor * gradient
    new_moment1 = 0.9 * moment1 + 0.1 * clipped
    new_moment2 = 0.95 * moment2 + 0.05 * clipped * clipped
    update = (new_moment1 / first_fix / (jnp.sqrt(new_moment2 / second_fix) + 1e-08)).astype(jnp.bfloat16)
    change = jnp.dot(projector, update, preferred_element_type=jnp.float32)
    new_weight = (weight.astype(jnp.float32) - 0.2 * change).astype(jnp.bfloat16)
    return (new_weight, new_moment1, new_moment2)
```

```python
import functools

import jax
import jax.numpy as jnp
from jax import lax
from jax.experimental import pallas as pl
from jax.experimental.pallas import tpu as pltpu
from jax.sharding import PartitionSpec as P


first_fix = 0.9999734386011124
second_fix = 0.994079470779666
RANK_CHUNKS = 4
COLUMN_CHUNKS = 2
F32 = jnp.float32
BF16 = jnp.bfloat16


def flip_pairs(n, bits):
    return [(i, i ^ bits) for i in range(n)]


def chunk_count(units, wanted):
    while units % wanted:
        wanted -= 1
    return wanted


def selection(rank, source):
    rows = lax.broadcasted_iota(jnp.int32, (rank, source.shape[0]), 0)
    return (rows == source[None, :]).astype(BF16)


def last_kernel(groups, basis_ref, *refs):
    parts, weight_ref, out_ref = refs[:groups], refs[groups], refs[-1]
    change = None
    update = jnp.concatenate([part[...] for part in parts], axis=0)
    change = jnp.dot(basis_ref[...], update, preferred_element_type=F32)
    out_ref[...] = (weight_ref[...].astype(F32) - 0.2 * change).astype(BF16)


def last_product(basis, parts, weight, before, start, width):
    rows, columns = weight.shape
    tile = chunk_tile(width)
    first = start // tile
    part_specs = [pl.BlockSpec((p.shape[0], tile), lambda i: (0, i)) for p in parts]
    there = pl.BlockSpec((rows, tile), lambda i: (0, i + first))
    in_specs = [pl.BlockSpec(basis.shape, lambda i: (0, 0)), *part_specs, there]
    args = [basis, *parts, weight]
    aliases = {}
    if before is not None:
        in_specs.append(pl.BlockSpec(memory_space=pl.ANY))
        aliases = {len(args): 0}
        args.append(before)
    return pl.pallas_call(
        functools.partial(last_kernel, len(parts)),
        grid=(width // tile,),
        in_specs=in_specs,
        out_specs=there,
        out_shape=jax.ShapeDtypeStruct((rows, columns), BF16),
        input_output_aliases=aliases,
    )(*args)


def chunk_tile(width):
    units = width // 128
    best = 1
    for n in range(1, 9):
        if units % n == 0:
            best = n
    return best * 128


def from_root(block, axis, holder):
    block = jnp.where(lax.axis_index(axis) == holder, block, jnp.zeros_like(block))
    return lax.psum(block, axis)


def body(dp, shard, acts, grad_out, projector, weight, moment1, moment2):
    rank = projector.shape[1]
    tokens = acts.shape[0]
    columns = grad_out.shape[1]
    own_rows = rank // dp
    depth = dp // 4
    chunks = chunk_count(max(own_rows // 8, 1), min(RANK_CHUNKS, max(own_rows // 8, 1)))
    piece = own_rows // chunks
    me = lax.axis_index("dp")
    core_pairs, x_pairs = flip_pairs(dp, 1), flip_pairs(dp, 2)
    z_pairs = [flip_pairs(dp, 4 * s) for s in range(depth)]
    place = jnp.arange(dp, dtype=jnp.int32)
    offset_bits = place // (2 * depth) + 2 * ((place // depth) % 2) + 4 * (place % depth)
    owner = me ^ offset_bits

    def hop(value, pairs):
        return lax.ppermute(value, "dp", pairs)

    def project(k):
        source = (owner[:, None] * own_rows + k * piece + jnp.arange(piece)[None, :]).reshape(-1)
        picked = jnp.dot(projector, selection(rank, source), preferred_element_type=F32).astype(BF16)
        return jnp.dot(acts, picked, preferred_element_type=F32)

    def complete(part):
        if shard == 2:
            other = lax.ppermute(part.astype(BF16), "shard", [(0, 1), (1, 0)])
            return (part + other.astype(F32)).astype(BF16)
        share = lax.psum_scatter(part, "shard", scatter_dimension=0, tiled=True).astype(BF16)
        return lax.all_gather(share, "shard", axis=0, tiled=True)

    def add(kept, received):
        return kept + received.astype(F32)

    def reduce_rows(part):
        half = part.shape[0] // 2
        part = add(part[:half], hop(part[half:].astype(BF16), core_pairs))
        half = half // 2
        part = add(part[:half], hop(part[half:].astype(BF16), x_pairs))
        total = part[:piece]
        for s in range(1, depth):
            total = add(total, hop(part[s * piece : (s + 1) * piece].astype(BF16), z_pairs[s]))
        return total

    grads = []
    for k in range(chunks):
        projected = complete(project(k))
        part = lax.dot_general(
            projected, grad_out, (((0,), (0,)), ((), ())), preferred_element_type=F32
        )
        grads.append(reduce_rows(part))
    gradient = jnp.concatenate(grads, axis=0)

    weight_rows = weight.shape[0]
    basis_count = projector.shape[0]
    holder = me * weight_rows // basis_count
    offset = me * weight_rows - holder * basis_count
    candidate = lax.dynamic_slice_in_dim(projector, offset, weight_rows, 0)
    if shard == 2:
        swapped = lax.ppermute(candidate, "shard", [(0, 1), (1, 0)])
        basis = jnp.where(lax.axis_index("shard") == holder, candidate, swapped)
    else:
        basis = from_root(candidate, "shard", holder)
    order = (owner[:, None] * own_rows + jnp.arange(own_rows)[None, :]).reshape(-1)
    basis = jnp.dot(basis, selection(rank, order), preferred_element_type=F32).astype(BF16)

    squares = jnp.sum(gradient * gradient).reshape(1, 1)
    squares = jnp.broadcast_to(squares, (8, 128))
    devices = dp * shard
    if shard == 2:
        def flips(bits):
            return lax.ppermute(squares, ("dp", "shard"), flip_pairs(devices, bits))

        squares = sum((flips(b) for b in range(1, 8)), squares)
        squares = sum((flips(8 * s) for s in range(1, depth)), squares)
    else:
        squares = lax.psum(squares, ("dp", "shard"))
    square_sum = squares[0, 0]
    whole = rank * columns * shard
    root_mean = jnp.sqrt(square_sum / whole + 1e-06)
    clip_factor = jnp.minimum(1.0, 4.0 / root_mean)

    clipped = clip_factor * gradient
    new_moment1 = 0.9 * moment1 + 0.1 * clipped
    new_moment2 = 0.95 * moment2 + 0.05 * clipped * clipped
    update = (new_moment1 / first_fix / (jnp.sqrt(new_moment2 / second_fix) + 1e-08)).astype(BF16)

    col_chunks = chunk_count(columns // 128, COLUMN_CHUNKS)
    width = columns // col_chunks
    new_weight = None
    for j in range(col_chunks):
        mine = update[:, j * width : (j + 1) * width]
        column_of_z = [mine] + [hop(mine, z_pairs[s]) for s in range(1, depth)]
        both_x = column_of_z + [hop(b, x_pairs) for b in column_of_z]
        parts = both_x + [hop(b, core_pairs) for b in both_x]
        new_weight = last_product(basis, parts, weight, new_weight, j * width, width)
    return (new_weight, new_moment1, new_moment2)


def solution(mesh):
    dp, shard = mesh.shape["dp"], mesh.shape["shard"]
    return jax.shard_map(
        functools.partial(body, dp, shard),
        mesh=mesh,
        in_specs=(
            P("dp", "shard"),
            P("dp", "shard"),
            P("shard", None),
            P("dp", "shard"),
            P("dp", "shard"),
            P("dp", "shard"),
        ),
        out_specs=(P("dp", "shard"), P("dp", "shard"), P("dp", "shard")),
        check_vma=False,
    )
```

```python
import functools

import jax
import jax.numpy as jnp
from jax import lax
from jax.experimental import pallas as pl
from jax.experimental.pallas import tpu as pltpu
from jax.sharding import PartitionSpec as P


first_fix = 0.9999734386011124
second_fix = 0.994079470779666
PROJECTION_TILE = 512
LAST_UNITS = 14
RANK_PARTS = (1, 2, 1)
COLUMN_PARTS = (1, 2, 2)
UPDATE_PARTS = (3, 3, 1)
LAST_ORDER = (0, 1, 2)
PIPELINE = (
    (0, 0), (0, 1), (1, 0), (0, 2), (1, 1), (2, 0), (0, 3), (3, 0),
    (2, 1), (4, 0), (3, 1), (1, 2), (4, 1), (0, 4), (2, 2), (1, 3),
    (3, 2), (4, 2), (2, 3), (1, 4), (3, 3), (4, 3), (2, 4), (3, 4),
    (4, 4),
)
F32 = jnp.float32
BF16 = jnp.bfloat16


def flip_pairs(n, bits):
    return [(i, i ^ bits) for i in range(n)]


def chunk_count(units, wanted):
    while units % wanted:
        wanted -= 1
    return wanted


def selection(rank, source):
    rows = lax.broadcasted_iota(jnp.int32, (rank, source.shape[0]), 0)
    return (rows == source[None, :]).astype(BF16)


def last_kernel(groups, basis_ref, *refs):
    parts, weight_ref, out_ref = refs[:groups], refs[groups], refs[-1]
    change = None
    update = jnp.concatenate([part[...] for part in parts], axis=0)
    change = jnp.dot(basis_ref[...], update, preferred_element_type=F32)
    out_ref[...] = (weight_ref[...].astype(F32) - 0.2 * change).astype(BF16)


def last_product(basis, parts, weight, before, start, width):
    rows, columns = weight.shape
    tile = chunk_tile(width, LAST_UNITS)
    first = start // tile
    part_specs = [pl.BlockSpec((p.shape[0], tile), lambda i: (0, i)) for p in parts]
    there = pl.BlockSpec((rows, tile), lambda i: (0, i + first))
    in_specs = [pl.BlockSpec(basis.shape, lambda i: (0, 0)), *part_specs, there]
    args = [basis, *parts, weight]
    aliases = {}
    if before is not None:
        in_specs.append(pl.BlockSpec(memory_space=pl.ANY))
        aliases = {len(args): 0}
        args.append(before)
    return pl.pallas_call(
        functools.partial(last_kernel, len(parts)),
        grid=(width // tile,),
        in_specs=in_specs,
        out_specs=there,
        out_shape=jax.ShapeDtypeStruct((rows, columns), BF16),
        input_output_aliases=aliases,
    )(*args)


def chunk_tile(width, most):
    units = width // 128
    best = 1
    for n in range(1, most + 1):
        if units % n == 0:
            best = n
    return best * 128


def from_root(block, axis, holder):
    block = jnp.where(lax.axis_index(axis) == holder, block, jnp.zeros_like(block))
    return lax.psum(block, axis)


def projection_kernel(counts, pick_ref, projector_ref, acts_ref, *refs):
    outs, picked = refs[:-1], refs[-1]

    @pl.when(pl.program_id(0) == 0)
    def _():
        picked[...] = lax.dot_general(
            pick_ref[...],
            projector_ref[...],
            (((1,), (1,)), ((), ())),
            preferred_element_type=F32,
        ).astype(BF16)

    part = lax.dot_general(
        picked[...], acts_ref[...], (((1,), (1,)), ((), ())), preferred_element_type=F32
    )
    first = 0
    for i, n in enumerate(counts):
        outs[2 * i][...] = part[first : first + n]
        outs[2 * i + 1][...] = part[first : first + n].astype(BF16)
        first += n


def projections(pick, projector, acts, counts, part=0, of=1):
    tokens, features = acts.shape[0] // of, acts.shape[1]
    tile = min(PROJECTION_TILE, tokens)
    first = part * (tokens // tile)
    shapes, specs = [], []
    for n in counts:
        for dtype in (F32, BF16):
            shapes.append(jax.ShapeDtypeStruct((n, tokens), dtype))
            specs.append(pl.BlockSpec((n, tile), lambda i: (0, i)))
    outs = pl.pallas_call(
        functools.partial(projection_kernel, counts),
        grid=(tokens // tile,),
        in_specs=[
            pl.BlockSpec(pick.shape, lambda i: (0, 0), pipeline_mode=pl.Buffered(1)),
            pl.BlockSpec(projector.shape, lambda i: (0, 0), pipeline_mode=pl.Buffered(1)),
            pl.BlockSpec((tile, features), lambda i: (i + first, 0)),
        ],
        out_specs=specs,
        out_shape=shapes,
        scratch_shapes=[pltpu.VMEM((pick.shape[0], features), BF16)],
    )(pick, projector, acts)
    return list(zip(outs[::2], outs[1::2]))


def halve(kept, received):
    total = kept + received.astype(F32)
    half = total.shape[0] // 2
    return total[:half], total[half:].astype(BF16)


def gradient_part(projected, grad_out, start, width):
    half = projected.shape[0] // 2
    part = jnp.dot(
        projected, grad_out[:, start : start + width], preferred_element_type=F32
    )
    return part[:half], part[half:].astype(BF16)


def after(value, *others):
    return lax.optimization_barrier((value, *others))[0] if others else value


def body(dp, shard, acts, grad_out, projector, weight, moment1, moment2):
    rank = projector.shape[1]
    columns = grad_out.shape[1]
    own_rows = rank // dp
    depth = dp // 4
    bits = dp.bit_length() - 1
    me = lax.axis_index("dp")
    pairs = [flip_pairs(dp, 1 << b) for b in range(bits)]
    place = jnp.arange(dp, dtype=jnp.int32)
    owner = me ^ sum(((place >> (bits - 1 - b)) & 1) << b for b in range(bits))

    def hop(value, stage):
        return lax.ppermute(value, "dp", pairs[stage])

    def fetch(part, sent):
        if shard == 2:
            return lax.ppermute(sent, "shard", [(0, 1), (1, 0)])
        share = lax.psum_scatter(part, "shard", scatter_dimension=1, tiled=True).astype(BF16)
        return lax.all_gather(share, "shard", axis=1, tiled=True)

    def complete(own, other, gate):
        other = after(other, *gate)
        return other if shard > 2 else (own + other.astype(F32)).astype(BF16)

    parts, splits = RANK_PARTS, COLUMN_PARTS
    if own_rows % sum(parts) or own_rows // sum(parts) < 8:
        parts, splits = (1,), (2,)
    unit_rows = own_rows // sum(parts)
    sources = []
    first = 0
    for n in parts:
        rows = owner[:, None] * own_rows + first + jnp.arange(n * unit_rows)[None, :]
        sources.append(rows.reshape(-1))
        first += n * unit_rows

    def one_hot(source):
        columns_at = lax.broadcasted_iota(jnp.int32, (source.shape[0], rank), 1)
        return (source[:, None] == columns_at).astype(BF16)

    halves = 1
    firsts, token = [], []
    for h in range(halves):
        pick = after(one_hot(sources[0]), *token)
        firsts += projections(pick, projector, acts, [sources[0].shape[0]], h, halves)
        token = firsts[-1]
    parts_sent = [firsts[0]]
    if len(sources) > 1:
        rest = after(one_hot(jnp.concatenate(sources[1:])), *token)
        parts_sent += projections(rest, projector, acts, [r.shape[0] for r in sources[1:]])

    weight_rows = weight.shape[0]
    basis_count = projector.shape[0]
    holder = me * weight_rows // basis_count
    offset = me * weight_rows - holder * basis_count
    candidate = lax.dynamic_slice_in_dim(projector, offset, weight_rows, 0)
    swapped = candidate
    if shard == 2:
        swapped = lax.ppermute(candidate, "shard", [(0, 1), (1, 0)])

    def own_basis(ready):
        if shard == 2:
            mine, theirs = lax.optimization_barrier((candidate, swapped, ready))[:2]
            basis = jnp.where(lax.axis_index("shard") == holder, mine, theirs)
        else:
            basis = from_root(candidate, "shard", holder)

        def z_before(s):
            return (me // 4 + depth - s) % depth * 4 + me % 4

        order_z = jnp.stack([z_before(s) for s in range(depth)])
        later = jnp.concatenate(
            [jnp.stack([order_z ^ c, order_z ^ (2 + c)], axis=1).reshape(-1) for c in (0, 1)]
        )
        order = (later[:, None] * own_rows + jnp.arange(own_rows)[None, :]).reshape(-1)
        return jnp.dot(basis, selection(rank, order), preferred_element_type=F32).astype(BF16)

    units = []
    for chunk, n in enumerate(parts):
        pieces = chunk_count(columns // 128, splits[chunk])
        for p in range(pieces):
            units.append((chunk, p * (columns // pieces), columns // pieces))
    fetched = [fetch(*part) for part in firsts]
    fetched = [fetched] + [[fetch(*p)] for i, p in enumerate(parts_sent) if i]
    parts_own = [[p[0] for p in firsts]] + [[p[0]] for p in parts_sent[1:]]
    steps = PIPELINE
    if len(units) != 5 or bits != 4:
        steps = [(i, stage) for i in range(len(units)) for stage in range(bits + 1)]
    sums, state, gate = {}, {}, [p for pair in parts_sent[1:] for p in pair]
    for i, stage in steps:
        if stage == 0:
            chunk, start, width = units[i]
            if chunk not in sums:
                both = zip(parts_own[chunk], fetched[chunk])
                sums[chunk] = jnp.concatenate([complete(a, b, gate) for a, b in both], axis=1)
                gate = []
            kept, sent = gradient_part(after(sums[chunk], *gate), grad_out, start, width)
            if i == len(units) - 1:
                basis = own_basis(sent)
        else:
            kept, received = state[i]
            if (i, stage) == steps[-2]:
                gate.append(basis)
            received = after(received, *gate)
            if stage == bits:
                state[i] = kept + received.astype(F32)
                gate = [state[i]]
                continue
            kept, sent = halve(kept, received)
        gate = [sent]
        state[i] = (kept, hop(sent, stage))
    done = [state[i] for i in range(len(units))]
    rows = []
    for chunk in range(len(parts)):
        rows.append(jnp.concatenate([d for d, u in zip(done, units) if u[0] == chunk], axis=1))
    gradient = jnp.concatenate(rows, axis=0)

    squares = jnp.sum(gradient * gradient).reshape(1, 1)
    squares = jnp.broadcast_to(squares, (8, 128))
    devices = dp * shard
    if shard == 2:
        everywhere = jnp.broadcast_to(squares[None], (devices, 8, 128))
        squares = lax.all_to_all(everywhere, ("dp", "shard"), 0, 0, tiled=True).sum(0)
    else:
        squares = lax.psum(squares, ("dp", "shard"))
    square_sum = squares[0, 0]
    whole = rank * columns * shard
    root_mean = jnp.sqrt(square_sum / whole + 1e-06)
    clip_factor = jnp.minimum(1.0, 4.0 / root_mean)

    clipped = clip_factor * gradient
    new_moment1 = 0.9 * moment1 + 0.1 * clipped
    new_moment2 = 0.95 * moment2 + 0.05 * clipped * clipped
    update = (new_moment1 / first_fix / (jnp.sqrt(new_moment2 / second_fix) + 1e-08)).astype(BF16)

    ring = [(i, (i + 4) % dp) for i in range(dp)]
    new_weight = None
    shares = UPDATE_PARTS if columns % (128 * sum(UPDATE_PARTS)) == 0 else (1,)
    for j, share in sorted(enumerate(shares), key=lambda part: LAST_ORDER[part[0]]):
        start = columns // sum(shares) * sum(shares[:j])
        width = columns // sum(shares) * share
        mine = update[:, start : start + width]
        blocks = []
        if j == 2:
            other = hop(mine, 1)
            blocks.append(jnp.concatenate([mine, other], axis=0))
            for _ in range(1, depth):
                blocks.append(lax.ppermute(blocks[-1], "dp", ring))
        else:
            for s in range(depth):
                if s:
                    mine = lax.ppermute(mine, "dp", ring)
                blocks += [mine, hop(mine, 1)]
        for block in list(blocks):
            blocks.append(hop(block, 0))
        new_weight = last_product(basis, blocks, weight, new_weight, start, width)
    return (new_weight, new_moment1, new_moment2)


def solution(mesh):
    dp, shard = mesh.shape["dp"], mesh.shape["shard"]

    def step(*args):
        return body(dp, shard, *args)

    return jax.shard_map(
        step,
        mesh=mesh,
        in_specs=(
            P("dp", "shard"),
            P("dp", "shard"),
            P("shard", None),
            P("dp", "shard"),
            P("dp", "shard"),
            P("dp", "shard"),
        ),
        out_specs=(P("dp", "shard"), P("dp", "shard"), P("dp", "shard")),
        check_vma=False,
    )
```

```python
import functools

import jax
import jax.numpy as jnp
from jax import lax
from jax.experimental import pallas as pl
from jax.experimental.pallas import tpu as pltpu
from jax.sharding import PartitionSpec as P


first_fix = 0.9999734386011124
second_fix = 0.994079470779666
PROJECTION_TILE = 1024
LAST_UNITS = 14
RANK_PARTS = (1, 2, 1)
COLUMN_PARTS = (1, 2, 2)
UPDATE_PARTS = (3, 3, 1)
LAST_ORDER = (0, 1, 2)
PIPELINE = (
    (0, 0), (0, 1), (1, 0), (0, 2), (1, 1), (2, 0), (0, 3), (3, 0),
    (2, 1), (4, 0), (3, 1), (1, 2), (4, 1), (0, 4), (2, 2), (1, 3),
    (3, 2), (4, 2), (2, 3), (1, 4), (3, 3), (4, 3), (2, 4), (3, 4),
    (4, 4),
)
F32 = jnp.float32
BF16 = jnp.bfloat16


def flip_pairs(n, bits):
    return [(i, i ^ bits) for i in range(n)]


def chunk_count(units, wanted):
    while units % wanted:
        wanted -= 1
    return wanted


def selection(rank, source):
    rows = lax.broadcasted_iota(jnp.int32, (rank, source.shape[0]), 0)
    return (rows == source[None, :]).astype(BF16)


def last_kernel(groups, basis_ref, *refs):
    parts, weight_ref, out_ref = refs[:groups], refs[groups], refs[-1]
    change = None
    update = jnp.concatenate([part[...] for part in parts], axis=0)
    change = jnp.dot(basis_ref[...], update, preferred_element_type=F32)
    out_ref[...] = (weight_ref[...].astype(F32) - 0.2 * change).astype(BF16)


def last_product(basis, parts, weight, before, start, width):
    rows, columns = weight.shape
    tile = chunk_tile(width, LAST_UNITS)
    first = start // tile
    part_specs = [pl.BlockSpec((p.shape[0], tile), lambda i: (0, i)) for p in parts]
    there = pl.BlockSpec((rows, tile), lambda i: (0, i + first))
    in_specs = [pl.BlockSpec(basis.shape, lambda i: (0, 0)), *part_specs, there]
    args = [basis, *parts, weight]
    aliases = {}
    if before is not None:
        in_specs.append(pl.BlockSpec(memory_space=pl.ANY))
        aliases = {len(args): 0}
        args.append(before)
    return pl.pallas_call(
        functools.partial(last_kernel, len(parts)),
        grid=(width // tile,),
        in_specs=in_specs,
        out_specs=there,
        out_shape=jax.ShapeDtypeStruct((rows, columns), BF16),
        input_output_aliases=aliases,
    )(*args)


def chunk_tile(width, most):
    units = width // 128
    best = 1
    for n in range(1, most + 1):
        if units % n == 0:
            best = n
    return best * 128


def from_root(block, axis, holder):
    block = jnp.where(lax.axis_index(axis) == holder, block, jnp.zeros_like(block))
    return lax.psum(block, axis)


def projection_kernel(counts, pick_ref, projector_ref, acts_ref, *refs):
    outs, picked = refs[:-1], refs[-1]

    @pl.when(pl.program_id(0) == 0)
    def _():
        picked[...] = lax.dot_general(
            pick_ref[...],
            projector_ref[...],
            (((1,), (1,)), ((), ())),
            preferred_element_type=F32,
        ).astype(BF16)

    part = lax.dot_general(
        picked[...], acts_ref[...], (((1,), (1,)), ((), ())), preferred_element_type=F32
    )
    first = 0
    for i, n in enumerate(counts):
        outs[2 * i][...] = part[first : first + n]
        outs[2 * i + 1][...] = part[first : first + n].astype(BF16)
        first += n


def projections(pick, projector, acts, counts, part=0, of=1):
    tokens, features = acts.shape[0] // of, acts.shape[1]
    tile = min(PROJECTION_TILE, tokens)
    first = part * (tokens // tile)
    shapes, specs = [], []
    for n in counts:
        for dtype in (F32, BF16):
            shapes.append(jax.ShapeDtypeStruct((n, tokens), dtype))
            specs.append(pl.BlockSpec((n, tile), lambda i: (0, i)))
    outs = pl.pallas_call(
        functools.partial(projection_kernel, counts),
        grid=(tokens // tile,),
        in_specs=[
            pl.BlockSpec(pick.shape, lambda i: (0, 0), pipeline_mode=pl.Buffered(1)),
            pl.BlockSpec(projector.shape, lambda i: (0, 0), pipeline_mode=pl.Buffered(1)),
            pl.BlockSpec((tile, features), lambda i: (i + first, 0)),
        ],
        out_specs=specs,
        out_shape=shapes,
        scratch_shapes=[pltpu.VMEM((pick.shape[0], features), BF16)],
    )(pick, projector, acts)
    return list(zip(outs[::2], outs[1::2]))


def halve(kept, received):
    total = kept + received.astype(F32)
    half = total.shape[0] // 2
    return total[:half], total[half:].astype(BF16)


def gradient_part(projected, grad_out, start, width):
    half = projected.shape[0] // 2
    part = jnp.dot(
        projected, grad_out[:, start : start + width], preferred_element_type=F32
    )
    return part[:half], part[half:].astype(BF16)


def after(value, *others):
    return lax.optimization_barrier((value, *others))[0] if others else value


def body(dp, shard, acts, grad_out, projector, weight, moment1, moment2):
    rank = projector.shape[1]
    columns = grad_out.shape[1]
    own_rows = rank // dp
    depth = dp // 4
    bits = dp.bit_length() - 1
    me = lax.axis_index("dp")
    pairs = [flip_pairs(dp, 1 << b) for b in range(bits)]
    place = jnp.arange(dp, dtype=jnp.int32)
    owner = me ^ sum(((place >> (bits - 1 - b)) & 1) << b for b in range(bits))

    def hop(value, stage):
        return lax.ppermute(value, "dp", pairs[stage])

    def fetch(part, sent):
        if shard == 2:
            return lax.ppermute(sent, "shard", [(0, 1), (1, 0)])
        share = lax.psum_scatter(part, "shard", scatter_dimension=1, tiled=True).astype(BF16)
        return lax.all_gather(share, "shard", axis=1, tiled=True)

    def complete(own, other, gate):
        other = after(other, *gate)
        return other if shard > 2 else (own + other.astype(F32)).astype(BF16)

    parts, splits = RANK_PARTS, COLUMN_PARTS
    if own_rows % sum(parts) or own_rows // sum(parts) < 8:
        parts, splits = (1,), (2,)
    unit_rows = own_rows // sum(parts)
    sources = []
    first = 0
    for n in parts:
        rows = owner[:, None] * own_rows + first + jnp.arange(n * unit_rows)[None, :]
        sources.append(rows.reshape(-1))
        first += n * unit_rows

    def one_hot(source):
        columns_at = lax.broadcasted_iota(jnp.int32, (source.shape[0], rank), 1)
        return (source[:, None] == columns_at).astype(BF16)

    halves = 1
    firsts, token = [], []
    for h in range(halves):
        pick = after(one_hot(sources[0]), *token)
        firsts += projections(pick, projector, acts, [sources[0].shape[0]], h, halves)
        token = firsts[-1]
    parts_sent = [firsts[0]]
    if len(sources) > 1:
        rest = after(one_hot(jnp.concatenate(sources[1:])), *token)
        parts_sent += projections(rest, projector, acts, [r.shape[0] for r in sources[1:]])

    weight_rows = weight.shape[0]
    basis_count = projector.shape[0]
    holder = me * weight_rows // basis_count
    offset = me * weight_rows - holder * basis_count
    candidate = lax.dynamic_slice_in_dim(projector, offset, weight_rows, 0)
    swapped = candidate
    if shard == 2:
        swapped = lax.ppermute(candidate, "shard", [(0, 1), (1, 0)])

    def own_basis(ready):
        if shard == 2:
            mine, theirs = lax.optimization_barrier((candidate, swapped, ready))[:2]
            basis = jnp.where(lax.axis_index("shard") == holder, mine, theirs)
        else:
            basis = from_root(candidate, "shard", holder)

        def z_before(s):
            return (me // 4 + depth - s) % depth * 4 + me % 4

        order_z = jnp.stack([z_before(s) for s in range(depth)])
        later = jnp.concatenate(
            [jnp.stack([order_z ^ c, order_z ^ (2 + c)], axis=1).reshape(-1) for c in (0, 1)]
        )
        order = (later[:, None] * own_rows + jnp.arange(own_rows)[None, :]).reshape(-1)
        return jnp.dot(basis, selection(rank, order), preferred_element_type=F32).astype(BF16)

    units = []
    for chunk, n in enumerate(parts):
        pieces = chunk_count(columns // 128, splits[chunk])
        for p in range(pieces):
            units.append((chunk, p * (columns // pieces), columns // pieces))
    fetched = [fetch(*part) for part in firsts]
    fetched = [fetched] + [[fetch(*p)] for i, p in enumerate(parts_sent) if i]
    parts_own = [[p[0] for p in firsts]] + [[p[0]] for p in parts_sent[1:]]
    steps = PIPELINE
    if len(units) != 5 or bits != 4:
        steps = [(i, stage) for i in range(len(units)) for stage in range(bits + 1)]
    sums, state, gate = {}, {}, [p for pair in parts_sent[1:] for p in pair]
    for i, stage in steps:
        if stage == 0:
            chunk, start, width = units[i]
            if chunk not in sums:
                both = zip(parts_own[chunk], fetched[chunk])
                sums[chunk] = jnp.concatenate([complete(a, b, gate) for a, b in both], axis=1)
                gate = []
            kept, sent = gradient_part(after(sums[chunk], *gate), grad_out, start, width)
            if i == len(units) - 1:
                basis = own_basis(sent)
        else:
            kept, received = state[i]
            if (i, stage) == steps[-2]:
                gate.append(basis)
            received = after(received, *gate)
            if stage == bits:
                state[i] = kept + received.astype(F32)
                gate = [state[i]]
                continue
            kept, sent = halve(kept, received)
        gate = [sent]
        state[i] = (kept, hop(sent, stage))
    done = [state[i] for i in range(len(units))]
    rows = []
    for chunk in range(len(parts)):
        rows.append(jnp.concatenate([d for d, u in zip(done, units) if u[0] == chunk], axis=1))
    gradient = jnp.concatenate(rows, axis=0)

    squares = (gradient * gradient).reshape(own_rows // 8, 8, columns // 128, 128).sum((0, 2))
    devices = dp * shard
    if shard == 2:
        everywhere = jnp.broadcast_to(squares[None], (devices, 8, 128))
        squares = lax.all_to_all(everywhere, ("dp", "shard"), 0, 0, tiled=True).sum(0)
    else:
        squares = lax.psum(squares, ("dp", "shard"))
    square_sum = jnp.sum(squares)
    whole = rank * columns * shard
    root_mean = jnp.sqrt(square_sum / whole + 1e-06)
    clip_factor = jnp.minimum(1.0, 4.0 / root_mean)

    clipped = clip_factor * gradient
    new_moment1 = 0.9 * moment1 + 0.1 * clipped
    new_moment2 = 0.95 * moment2 + 0.05 * clipped * clipped
    update = (new_moment1 / first_fix / (jnp.sqrt(new_moment2 / second_fix) + 1e-08)).astype(BF16)

    ring = [(i, (i + 4) % dp) for i in range(dp)]
    new_weight = None
    shares = UPDATE_PARTS if columns % (128 * sum(UPDATE_PARTS)) == 0 else (1,)
    for j, share in sorted(enumerate(shares), key=lambda part: LAST_ORDER[part[0]]):
        start = columns // sum(shares) * sum(shares[:j])
        width = columns // sum(shares) * share
        mine = update[:, start : start + width]
        blocks = []
        if j == 2:
            other = hop(mine, 1)
            blocks.append(jnp.concatenate([mine, other], axis=0))
            for _ in range(1, depth):
                blocks.append(lax.ppermute(blocks[-1], "dp", ring))
        else:
            for s in range(depth):
                if s:
                    mine = lax.ppermute(mine, "dp", ring)
                blocks += [mine, hop(mine, 1)]
        for block in list(blocks):
            blocks.append(hop(block, 0))
        new_weight = last_product(basis, blocks, weight, new_weight, start, width)
    return (new_weight, new_moment1, new_moment2)


def solution(mesh):
    dp, shard = mesh.shape["dp"], mesh.shape["shard"]

    def step(*args):
        return body(dp, shard, *args)

    return jax.shard_map(
        step,
        mesh=mesh,
        in_specs=(
            P("dp", "shard"),
            P("dp", "shard"),
            P("shard", None),
            P("dp", "shard"),
            P("dp", "shard"),
            P("dp", "shard"),
        ),
        out_specs=(P("dp", "shard"), P("dp", "shard"), P("dp", "shard")),
        check_vma=False,
    )
```
